32 devices in a mesh: groups: 2 (over y), row: 4 (over z), col: 4 (over x, core).
Axes of the slice: x: 2, y: 2, z: 4, core: 2. Of those that a mesh axis runs over, the one named last changes fastest.
Arguments:
- integrals: float32 [32, 16, 512], P('groups', ('row', 'col')), parts along dimension 0, may hold values from -6 to 6
- occupied: float32 [32, 16], P('groups'), parts along dimension 0, may hold values from -1.5 to 1.5
- virtual: float32 [32, 16], P('groups'), parts along dimension 0, may hold values from -1.5 to 1.5
- int_mask: int32 [8, 16, 8], P('groups', ('row', 'col')), parts along dimension 0, may hold values 0 or 1
- occ_mask: int32 [8, 4], P('groups'), parts along dimension 0, may hold values 0 or 1
- virt_mask: int32 [8, 4], P('groups'), parts along dimension 0, may hold values 0 or 1
Outputs:
- polarizability: float32 [1024, 512], P(('groups', 'row')), parts along dimension 0
The draws below stay inside these ranges and needn't reach their ends.
There are 2 independent parts, one for each index of `groups`. The reference program is written for one: setup_inputs(seed, part) draws one part's arguments, and reference() takes and returns one part's arrays. A program takes and returns all parts, laid end to end along the dimension named above; each array names one. Nothing has to cross between parts.
All inputs are finite; a program needn't handle non-finite values. No bound on the sum of `int_mask` on one device may be relied on, other than what follows from the above.
Results may differ from the reference program's by a relative error of at most 0.0001.
Values sent between devices are 32-bit elements; how exact they have to be, the bound alone decides.
A program may use at most 64 MiB of HBM per device.

```python
import jax
import jax.numpy as jnp
from jax import lax

NAUX = 512
ATILE = 64
NB = 16
GTILE = 4


def touch_ends(values, stream_key, smallest, largest):
    shape = values.shape
    spot = [jax.random.randint(jax.random.fold_in(stream_key, axis), (), 0, shape[axis]) for axis in range(len(shape))]
    values = values.at[tuple(spot)].set(smallest)
    longest = shape.index(max(shape))
    spot[longest] = (spot[longest] + 1) % shape[longest]
    return values.at[tuple(spot)].set(largest)


def shard_levels(key, extent, pieces, low, top_value):
    def one(dim, blocks):
        steps = jax.random.uniform(jax.random.fold_in(jax.random.fold_in(key, 6), dim), (blocks,), jnp.float32, low / len(pieces), top_value / len(pieces))
        return jnp.repeat(jnp.exp(steps), extent[dim] // blocks).reshape((-1,) + (1,) * (len(extent) - dim - 1))

    loudness = one(*pieces[0])
    for cut in pieces[1:]:
        loudness = loudness * one(*cut)
    return loudness


def bell_draw(stream_key, dims, scale, limit, cuts=(), held_as=jnp.bfloat16):
    factor_of = shard_levels(stream_key, dims, cuts, -0.22, 0.18) if cuts else 1.0
    entries = jax.random.normal(stream_key, dims, jnp.float32) * scale * factor_of
    return jnp.minimum(jnp.maximum(entries, -limit), limit).astype(held_as)


def setup_inputs(seed: int = 0, part: int = 0) -> dict:
    arg_keys = jax.random.split(jax.random.key(seed), 7)
    own_keys = jax.random.split(jax.random.fold_in(arg_keys[6], part), 7)
    integrals = bell_draw(own_keys[0], (NB, NB, NAUX), 1.0, 6.0, ((1, 16),), jnp.float32)
    occupied = bell_draw(own_keys[1], (NB, NB), NB ** -0.5, 1.5, (), jnp.float32)
    virtual = bell_draw(own_keys[2], (NB, NB), NB ** -0.5, 1.5, (), jnp.float32)
    int_mask = touch_ends((jax.random.randint(own_keys[3], (NB // GTILE, NB, NAUX // ATILE), 0, 4) < 3).astype(jnp.int32), jax.random.fold_in(own_keys[3], 1), 0, 1)
    occ_mask = touch_ends((jax.random.randint(own_keys[4], (NB // GTILE, NB // GTILE), 0, 3) < 2).astype(jnp.int32), jax.random.fold_in(own_keys[4], 1), 0, 1)
    virt_mask = touch_ends((jax.random.randint(own_keys[5], (NB // GTILE, NB // GTILE), 0, 3) < 2).astype(jnp.int32), jax.random.fold_in(own_keys[5], 1), 0, 1)
    return dict(integrals=integrals, occupied=occupied, virtual=virtual, int_mask=int_mask, occ_mask=occ_mask, virt_mask=virt_mask)


def spread_two(mask, tile_rows, tile_cols):
    outer, inner = mask.shape
    wide = jnp.broadcast_to(mask[:, None, :, None], (outer, tile_rows, inner, tile_cols))
    return wide.reshape(outer * tile_rows, inner * tile_cols).astype(jnp.float32)


def spread_three(mask, tile_rows, tile_cols):
    outer, middle, inner = mask.shape
    wide = jnp.broadcast_to(mask[:, None, :, :, None], (outer, tile_rows, middle, inner, tile_cols))
    return wide.reshape(outer * tile_rows, middle, inner * tile_cols).astype(jnp.float32)


def reference(integrals, occupied, virtual, int_mask, occ_mask, virt_mask):
    highest = lax.Precision.HIGHEST
    int_full = integrals * spread_three(int_mask, GTILE, ATILE)
    occ_full = occupied * spread_two(occ_mask, GTILE, GTILE)
    virt_full = virtual * spread_two(virt_mask, GTILE, GTILE)
    blocks = NB // GTILE

    def step(index, total):
        start = (index * GTILE).astype(jnp.int32)
        piece = lax.dynamic_slice_in_dim(int_full, start, GTILE, 1)
        occ_part = jnp.einsum("mn,mlp->nlp", occ_full, piece, precision=highest)
        virt_cols = lax.dynamic_slice_in_dim(virt_full, start, GTILE, 1)
        virt_part = jnp.einsum("sl,snq->nlq", virt_cols, int_full, precision=highest)
        return total + jnp.einsum("nlp,nlq->pq", occ_part, virt_part, precision=highest)

    total = lax.fori_loop(0, blocks, step, jnp.zeros((NAUX, NAUX), jnp.float32))
    return total / NB
```

```python
import functools

import jax
import jax.numpy as jnp
from jax import lax
from jax.experimental import pallas as pl
from jax.experimental.pallas import tpu as pltpu
from jax.sharding import PartitionSpec as P

MESH = pl.DeviceIdType.MESH


def spread_two(mask, tile_rows, tile_cols):
    outer, inner = mask.shape
    wide = jnp.broadcast_to(mask[:, None, :, None], (outer, tile_rows, inner, tile_cols))
    return wide.reshape(outer * tile_rows, inner * tile_cols).astype(jnp.float32)


def spread_three(mask, tile_rows, tile_cols):
    outer, middle, inner = mask.shape
    wide = jnp.broadcast_to(mask[:, None, :, :, None], (outer, tile_rows, middle, inner, tile_cols))
    return wide.reshape(outer * tile_rows, middle, inner * tile_cols).astype(jnp.float32)


def exchange_plan(integrals, occupied, virtual, int_mask, occ_mask, virt_mask):
    highest = lax.Precision.HIGHEST
    basis = occupied.shape[0]
    local_pairs = integrals.shape[1]
    aux_count = integrals.shape[2]
    green_tile = basis // occ_mask.shape[0]
    aux_tile = aux_count // int_mask.shape[2]
    row_count = lax.axis_size("row")
    col_count = lax.axis_size("col")
    int_full = integrals * spread_three(int_mask, green_tile, aux_tile)
    occ_full = occupied * spread_two(occ_mask, green_tile, green_tile)
    virt_full = virtual * spread_two(virt_mask, green_tile, green_tile)
    flat = int_full.reshape(basis, local_pairs * aux_count)
    contract_first = (((0,), (0,)), ((), ()))
    trans_virt = lax.dot_general(
        virt_full, flat, contract_first, precision=highest, preferred_element_type=jnp.float32
    )
    shaped_virt = trans_virt.reshape(row_count, col_count, local_pairs, local_pairs, aux_count)
    mirrored = lax.all_to_all(
        lax.all_to_all(shaped_virt, "row", split_axis=0, concat_axis=0, tiled=True),
        "col",
        split_axis=1,
        concat_axis=1,
        tiled=True,
    )
    trans_occ = lax.dot_general(
        occ_full, flat, contract_first, precision=highest, preferred_element_type=jnp.float32
    )
    shaped_occ = trans_occ.reshape(row_count, col_count, local_pairs, local_pairs, aux_count)
    pair_dims = (((0, 1, 2, 3), (0, 1, 3, 2)), ((), ()))
    whole = (
        lax.dot_general(
            shaped_occ, mirrored, pair_dims, precision=highest, preferred_element_type=jnp.float32
        )
        / basis
    )
    summed = lax.psum(whole, "col")
    return lax.psum_scatter(summed, "row", scatter_dimension=0, tiled=True)


def one_hot(shape, which):
    rows = lax.broadcasted_iota(jnp.int32, shape, 0)
    cols = lax.broadcasted_iota(jnp.int32, shape, 1)
    return jnp.where(which(rows, cols), 1.0, 0.0).astype(jnp.float32)


def dot(a, b, dims=(((1,), (0,)), ((), ())), precision=None):
    return lax.dot_general(a, b, dims, precision=precision, preferred_element_type=jnp.float32)


def spread_tiles(mask, tile_rows, tile_cols):
    outer, inner = mask.shape
    up = one_hot((outer * tile_rows, outer), lambda i, j: i // tile_rows == j)
    across = one_hot((inner, inner * tile_cols), lambda i, j: j // tile_cols == i)
    return dot(dot(up, mask.astype(jnp.float32)), across)


def split(x):
    high = x.astype(jnp.bfloat16)
    return high, (x - high.astype(jnp.float32)).astype(jnp.bfloat16)


def dot_three(a, b, dims=(((1,), (0,)), ((), ()))):
    (a_high, a_low), (b_high, b_low) = a, b
    return dot(a_high, b_high, dims) + (dot(a_high, b_low, dims) + dot(a_low, b_high, dims))


def gather_kernel(
    rows, cols, int_ref, occ_ref, virt_ref, imask_ref, omask_ref, vmask_ref, out_ref,
    held, pair_high, pair_low, send_sem, recv_sem
):
    basis, aux = int_ref.shape
    green_tile = basis // omask_ref.shape[0]
    highest = lax.Precision.HIGHEST
    group = lax.axis_index("groups")
    row = lax.axis_index("row")
    col = lax.axis_index("col")
    mate = col + 1 - 2 * (col % 2)
    across = (col + 2) % 4
    barrier = pltpu.get_barrier_semaphore()

    others = [lax.rem(row + d, rows) for d in range(1, rows)]
    peers = [(group, other, col) for other in others] + [(group, row, across), (group, row, mate)]
    for peer in peers:
        pl.semaphore_signal(barrier, inc=1, device_id=peer, device_id_type=MESH)

    mask = spread_tiles(imask_ref[...], green_tile, aux // imask_ref.shape[1])
    held[row * cols + col] = int_ref[...] * mask
    pl.semaphore_wait(barrier, len(peers))

    started = []

    def send(block, peer):
        copy = pltpu.make_async_remote_copy(
            src_ref=held.at[block],
            dst_ref=held.at[block],
            send_sem=send_sem.at[len(started)],
            recv_sem=recv_sem.at[block],
            device_id=peer,
            device_id_type=MESH,
        )
        copy.start()
        started.append(copy)

    def arrive(block):
        pltpu.make_async_remote_copy(
            src_ref=held.at[block],
            dst_ref=held.at[block],
            send_sem=send_sem.at[0],
            recv_sem=recv_sem.at[block],
            device_id=(group, row, mate),
            device_id_type=MESH,
        ).wait_recv()

    mine = row * cols + col
    for other in others:
        send(mine, (group, other, col))
    send(mine, (group, row, across))
    send(mine, (group, row, mate))

    occ = occ_ref[...] * spread_tiles(omask_ref[...], green_tile, green_tile)
    virt = virt_ref[...] * spread_tiles(vmask_ref[...], green_tile, green_tile)
    wide = (basis, basis * basis)
    occ_cols = dot(occ, one_hot(wide, lambda i, j: j // basis == i), precision=highest)
    virt_cols = dot(
        virt, one_hot(wide, lambda i, j: j % basis == i), (((0,), (0,)), ((), ())), precision=highest
    )
    pair = (occ_cols[None] * virt_cols[:, None]).reshape(basis * basis, basis * basis) / basis
    high, low = split(pair)
    pair_high[...] = high
    pair_low[...] = low

    arrive(row * cols + across)
    send(row * cols + across, (group, row, mate))
    for other in others:
        arrive(other * cols + col)
        send(other * cols + col, (group, row, across))
        send(other * cols + col, (group, row, mate))
    for other in others:
        arrive(other * cols + across)
        send(other * cols + across, (group, row, mate))
    arrive(row * cols + mate)
    far = across + 1 - 2 * (across % 2)
    arrive(row * cols + far)
    for other in others:
        arrive(other * cols + mate)
    for other in others:
        arrive(other * cols + far)
    for copy in started:
        copy.wait_send()

    mine_out = out_ref.shape[0]
    begin = pl.multiple_of(row * mine_out, mine_out)
    left = held[:, :, pl.ds(begin, mine_out)].reshape(basis * basis, mine_out)
    turned = dot_three(split(left.T), (pair_high[...], pair_low[...]))
    whole = split(held[...].reshape(basis * basis, aux))
    out_ref[...] = dot_three(split(turned), whole)


def gather_plan(integrals, occupied, virtual, int_mask, occ_mask, virt_mask):
    basis, _, aux = integrals.shape
    rows, cols = lax.axis_size("row"), lax.axis_size("col")
    vmem = pl.BlockSpec(memory_space=pltpu.VMEM)
    return pl.pallas_call(
        functools.partial(gather_kernel, rows, cols),
        out_shape=jax.ShapeDtypeStruct((aux // rows, aux), jnp.float32),
        in_specs=[vmem] * 6,
        out_specs=vmem,
        scratch_shapes=[
            pltpu.VMEM((basis, basis, aux), jnp.float32),
            pltpu.VMEM((basis * basis, basis * basis), jnp.bfloat16),
            pltpu.VMEM((basis * basis, basis * basis), jnp.bfloat16),
            pltpu.SemaphoreType.DMA((4 * rows,)),
            pltpu.SemaphoreType.DMA((rows * cols,)),
        ],
        compiler_params=pltpu.CompilerParams(collective_id=0, has_side_effects=True),
    )(
        integrals.reshape(basis, aux),
        occupied,
        virtual,
        int_mask.reshape(int_mask.shape[0], int_mask.shape[2]),
        occ_mask,
        virt_mask,
    )


def per_device(integrals, occupied, virtual, int_mask, occ_mask, virt_mask):
    basis, local_pairs, aux = integrals.shape
    rows, cols = lax.axis_size("row"), lax.axis_size("col")
    small = local_pairs == 1 and cols == 4 and rows * cols == basis
    fits = basis * basis * (aux + basis * basis) * 4 <= 16 * 1024 * 1024
    tiled = basis % 8 == 0 and aux % (128 * rows) == 0
    plan = gather_plan if small and fits and tiled else exchange_plan
    return plan(integrals, occupied, virtual, int_mask, occ_mask, virt_mask)


def solution(mesh):
    placed = (
        P("groups", ("row", "col"), None),
        P("groups", None),
        P("groups", None),
        P("groups", ("row", "col"), None),
        P("groups", None),
        P("groups", None),
    )
    return jax.shard_map(
        per_device,
        mesh=mesh,
        in_specs=placed,
        out_specs=P(("groups", "row"), None),
        check_vma=False,
    )
```

```python
import functools

import jax
import jax.numpy as jnp
from jax import lax
from jax.experimental import pallas as pl
from jax.experimental.pallas import tpu as pltpu
from jax.sharding import PartitionSpec as P

MESH = pl.DeviceIdType.MESH


def spread_two(mask, tile_rows, tile_cols):
    outer, inner = mask.shape
    wide = jnp.broadcast_to(mask[:, None, :, None], (outer, tile_rows, inner, tile_cols))
    return wide.reshape(outer * tile_rows, inner * tile_cols).astype(jnp.float32)


def spread_three(mask, tile_rows, tile_cols):
    outer, middle, inner = mask.shape
    wide = jnp.broadcast_to(mask[:, None, :, :, None], (outer, tile_rows, middle, inner, tile_cols))
    return wide.reshape(outer * tile_rows, middle, inner * tile_cols).astype(jnp.float32)


def exchange_plan(integrals, occupied, virtual, int_mask, occ_mask, virt_mask):
    highest = lax.Precision.HIGHEST
    basis = occupied.shape[0]
    local_pairs = integrals.shape[1]
    aux_count = integrals.shape[2]
    green_tile = basis // occ_mask.shape[0]
    aux_tile = aux_count // int_mask.shape[2]
    row_count = lax.axis_size("row")
    col_count = lax.axis_size("col")
    int_full = integrals * spread_three(int_mask, green_tile, aux_tile)
    occ_full = occupied * spread_two(occ_mask, green_tile, green_tile)
    virt_full = virtual * spread_two(virt_mask, green_tile, green_tile)
    flat = int_full.reshape(basis, local_pairs * aux_count)
    contract_first = (((0,), (0,)), ((), ()))
    trans_virt = lax.dot_general(
        virt_full, flat, contract_first, precision=highest, preferred_element_type=jnp.float32
    )
    shaped_virt = trans_virt.reshape(row_count, col_count, local_pairs, local_pairs, aux_count)
    mirrored = lax.all_to_all(
        lax.all_to_all(shaped_virt, "row", split_axis=0, concat_axis=0, tiled=True),
        "col",
        split_axis=1,
        concat_axis=1,
        tiled=True,
    )
    trans_occ = lax.dot_general(
        occ_full, flat, contract_first, precision=highest, preferred_element_type=jnp.float32
    )
    shaped_occ = trans_occ.reshape(row_count, col_count, local_pairs, local_pairs, aux_count)
    pair_dims = (((0, 1, 2, 3), (0, 1, 3, 2)), ((), ()))
    whole = (
        lax.dot_general(
            shaped_occ, mirrored, pair_dims, precision=highest, preferred_element_type=jnp.float32
        )
        / basis
    )
    summed = lax.psum(whole, "col")
    return lax.psum_scatter(summed, "row", scatter_dimension=0, tiled=True)


def one_hot(shape, which):
    rows = lax.broadcasted_iota(jnp.int32, shape, 0)
    cols = lax.broadcasted_iota(jnp.int32, shape, 1)
    return jnp.where(which(rows, cols), 1.0, 0.0).astype(jnp.float32)


def dot(a, b, dims=(((1,), (0,)), ((), ())), precision=None):
    return lax.dot_general(a, b, dims, precision=precision, preferred_element_type=jnp.float32)


def spread_tiles(mask, tile_rows, tile_cols):
    outer, inner = mask.shape
    up = one_hot((outer * tile_rows, outer), lambda i, j: i // tile_rows == j)
    across = one_hot((inner, inner * tile_cols), lambda i, j: j // tile_cols == i)
    return dot(dot(up, mask.astype(jnp.float32)), across)


def split(x):
    high = x.astype(jnp.bfloat16)
    return high, (x - high.astype(jnp.float32)).astype(jnp.bfloat16)


def dot_three(a, b, dims=(((1,), (0,)), ((), ()))):
    (a_high, a_low), (b_high, b_low) = a, b
    return dot(a_high, b_high, dims) + (dot(a_high, b_low, dims) + dot(a_low, b_high, dims))


def nearest_first(place, count):
    orders = [
        sorted((k for k in range(count) if k != at), key=lambda k: (abs(k - at), k))
        for at in range(count)
    ]
    steps = []
    for step in range(count - 1):
        other = orders[0][step]
        for at in range(1, count):
            other = jnp.where(place == at, orders[at][step], other)
        steps.append(other)
    return steps


def gather_kernel(
    rows, cols, int_hbm, occ_hbm, virt_hbm, imask_hbm, omask_hbm, vmask_hbm, out_ref,
    held, pair_high, pair_low, int_ref, occ_ref, virt_ref, imask_ref, omask_ref, vmask_ref,
    load_sem, send_sem, recv_sem
):
    basis, aux = int_ref.shape
    green_tile = basis // omask_ref.shape[0]
    highest = lax.Precision.HIGHEST
    group = lax.axis_index("groups")
    row = lax.axis_index("row")
    col = lax.axis_index("col")
    mate = col + 1 - 2 * (col % 2)
    across = (col + 2) % 4
    barrier = pltpu.get_barrier_semaphore()

    others = nearest_first(row, rows)
    peers = [(group, other, col) for other in others] + [(group, row, across), (group, row, mate)]
    for peer in peers:
        pl.semaphore_signal(barrier, inc=1, device_id=peer, device_id_type=MESH)

    sources = (imask_hbm.at[:, 0, :], int_hbm.at[:, 0, :], omask_hbm, vmask_hbm, occ_hbm, virt_hbm)
    targets = (imask_ref, int_ref, omask_ref, vmask_ref, occ_ref, virt_ref)
    loads = [
        pltpu.make_async_copy(source, target, load_sem.at[k])
        for k, (source, target) in enumerate(zip(sources, targets))
    ]
    for load in loads:
        load.start()
    loads[0].wait()
    mask = spread_tiles(imask_ref[...], green_tile, aux // imask_ref.shape[1])
    loads[1].wait()
    held[row * cols + col] = int_ref[...] * mask
    pl.semaphore_wait(barrier, len(peers))

    started = []

    def send(block, peer):
        copy = pltpu.make_async_remote_copy(
            src_ref=held.at[block],
            dst_ref=held.at[block],
            send_sem=send_sem.at[len(started)],
            recv_sem=recv_sem.at[block],
            device_id=peer,
            device_id_type=MESH,
        )
        copy.start()
        started.append(copy)

    def arrive(block):
        pltpu.make_async_remote_copy(
            src_ref=held.at[block],
            dst_ref=held.at[block],
            send_sem=send_sem.at[0],
            recv_sem=recv_sem.at[block],
            device_id=(group, row, mate),
            device_id_type=MESH,
        ).wait_recv()

    mine = row * cols + col
    for other in others:
        send(mine, (group, other, col))
    send(mine, (group, row, across))
    send(mine, (group, row, mate))

    for load in loads[2:]:
        load.wait()
    occ = occ_ref[...] * spread_tiles(omask_ref[...], green_tile, green_tile)
    virt = virt_ref[...] * spread_tiles(vmask_ref[...], green_tile, green_tile)
    wide = (basis, basis * basis)
    occ_cols = dot(occ, one_hot(wide, lambda i, j: j // basis == i), precision=highest)
    virt_cols = dot(
        virt, one_hot(wide, lambda i, j: j % basis == i), (((0,), (0,)), ((), ())), precision=highest
    )
    pair = (occ_cols[None] * virt_cols[:, None]).reshape(basis * basis, basis * basis) / basis
    high, low = split(pair)
    pair_high[...] = high
    pair_low[...] = low

    arrive(row * cols + across)
    send(row * cols + across, (group, row, mate))
    for other in others:
        arrive(other * cols + col)
        send(other * cols + col, (group, row, across))
        send(other * cols + col, (group, row, mate))
    for other in others:
        arrive(other * cols + across)
        send(other * cols + across, (group, row, mate))
    arrive(row * cols + mate)
    far = across + 1 - 2 * (across % 2)
    arrive(row * cols + far)
    for other in others:
        arrive(other * cols + mate)
    for other in others:
        arrive(other * cols + far)
    for copy in started:
        copy.wait_send()

    mine_out = out_ref.shape[0]
    begin = pl.multiple_of(row * mine_out, mine_out)
    left = held[:, :, pl.ds(begin, mine_out)].reshape(basis * basis, mine_out)
    turned = dot_three(split(left.T), (pair_high[...], pair_low[...]))
    whole = split(held[...].reshape(basis * basis, aux))
    out_ref[...] = dot_three(split(turned), whole)


def gather_plan(integrals, occupied, virtual, int_mask, occ_mask, virt_mask):
    basis, _, aux = integrals.shape
    rows, cols = lax.axis_size("row"), lax.axis_size("col")
    anywhere = pl.BlockSpec(memory_space=pl.ANY)
    return pl.pallas_call(
        functools.partial(gather_kernel, rows, cols),
        out_shape=pltpu.VMEM((aux // rows, aux), jnp.float32),
        in_specs=[anywhere] * 6,
        out_specs=pl.BlockSpec(memory_space=pltpu.VMEM),
        scratch_shapes=[
            pltpu.VMEM((basis, basis, aux), jnp.float32),
            pltpu.VMEM((basis * basis, basis * basis), jnp.bfloat16),
            pltpu.VMEM((basis * basis, basis * basis), jnp.bfloat16),
            pltpu.VMEM((basis, aux), jnp.float32),
            pltpu.VMEM(occupied.shape, jnp.float32),
            pltpu.VMEM(virtual.shape, jnp.float32),
            pltpu.VMEM((int_mask.shape[0], int_mask.shape[2]), jnp.int32),
            pltpu.VMEM(occ_mask.shape, jnp.int32),
            pltpu.VMEM(virt_mask.shape, jnp.int32),
            pltpu.SemaphoreType.DMA((6,)),
            pltpu.SemaphoreType.DMA((4 * rows,)),
            pltpu.SemaphoreType.DMA((rows * cols,)),
        ],
        compiler_params=pltpu.CompilerParams(collective_id=0, has_side_effects=True),
    )(integrals, occupied, virtual, int_mask, occ_mask, virt_mask)


def per_device(integrals, occupied, virtual, int_mask, occ_mask, virt_mask):
    basis, local_pairs, aux = integrals.shape
    rows, cols = lax.axis_size("row"), lax.axis_size("col")
    small = local_pairs == 1 and cols == 4 and rows * cols == basis
    fits = basis * basis * (aux + basis * basis) * 4 <= 16 * 1024 * 1024
    tiled = basis % 8 == 0 and aux % (128 * rows) == 0
    plan = gather_plan if small and fits and tiled else exchange_plan
    return plan(integrals, occupied, virtual, int_mask, occ_mask, virt_mask)


def solution(mesh):
    placed = (
        P("groups", ("row", "col"), None),
        P("groups", None),
        P("groups", None),
        P("groups", ("row", "col"), None),
        P("groups", None),
        P("groups", None),
    )
    return jax.shard_map(
        per_device,
        mesh=mesh,
        in_specs=placed,
        out_specs=P(("groups", "row"), None),
        check_vma=False,
    )
```

```python
import functools

import jax
import jax.numpy as jnp
from jax import lax
from jax.experimental import pallas as pl
from jax.experimental.pallas import tpu as pltpu
from jax.sharding import PartitionSpec as P

MESH = pl.DeviceIdType.MESH


def spread_two(mask, tile_rows, tile_cols):
    outer, inner = mask.shape
    wide = jnp.broadcast_to(mask[:, None, :, None], (outer, tile_rows, inner, tile_cols))
    return wide.reshape(outer * tile_rows, inner * tile_cols).astype(jnp.float32)


def spread_three(mask, tile_rows, tile_cols):
    outer, middle, inner = mask.shape
    wide = jnp.broadcast_to(mask[:, None, :, :, None], (outer, tile_rows, middle, inner, tile_cols))
    return wide.reshape(outer * tile_rows, middle, inner * tile_cols).astype(jnp.float32)


def exchange_plan(integrals, occupied, virtual, int_mask, occ_mask, virt_mask):
    highest = lax.Precision.HIGHEST
    basis = occupied.shape[0]
    local_pairs = integrals.shape[1]
    aux_count = integrals.shape[2]
    green_tile = basis // occ_mask.shape[0]
    aux_tile = aux_count // int_mask.shape[2]
    row_count = lax.axis_size("row")
    col_count = lax.axis_size("col")
    int_full = integrals * spread_three(int_mask, green_tile, aux_tile)
    occ_full = occupied * spread_two(occ_mask, green_tile, green_tile)
    virt_full = virtual * spread_two(virt_mask, green_tile, green_tile)
    flat = int_full.reshape(basis, local_pairs * aux_count)
    contract_first = (((0,), (0,)), ((), ()))
    trans_virt = lax.dot_general(
        virt_full, flat, contract_first, precision=highest, preferred_element_type=jnp.float32
    )
    shaped_virt = trans_virt.reshape(row_count, col_count, local_pairs, local_pairs, aux_count)
    mirrored = lax.all_to_all(
        lax.all_to_all(shaped_virt, "row", split_axis=0, concat_axis=0, tiled=True),
        "col",
        split_axis=1,
        concat_axis=1,
        tiled=True,
    )
    trans_occ = lax.dot_general(
        occ_full, flat, contract_first, precision=highest, preferred_element_type=jnp.float32
    )
    shaped_occ = trans_occ.reshape(row_count, col_count, local_pairs, local_pairs, aux_count)
    pair_dims = (((0, 1, 2, 3), (0, 1, 3, 2)), ((), ()))
    whole = (
        lax.dot_general(
            shaped_occ, mirrored, pair_dims, precision=highest, preferred_element_type=jnp.float32
        )
        / basis
    )
    summed = lax.psum(whole, "col")
    return lax.psum_scatter(summed, "row", scatter_dimension=0, tiled=True)


def one_hot(shape, which):
    rows = lax.broadcasted_iota(jnp.int32, shape, 0)
    cols = lax.broadcasted_iota(jnp.int32, shape, 1)
    return jnp.where(which(rows, cols), 1.0, 0.0).astype(jnp.float32)


def dot(a, b, dims=(((1,), (0,)), ((), ())), precision=None):
    return lax.dot_general(a, b, dims, precision=precision, preferred_element_type=jnp.float32)


def spread_tiles(mask, tile_rows, tile_cols):
    outer, inner = mask.shape
    up = one_hot((outer * tile_rows, outer), lambda i, j: i // tile_rows == j)
    across = one_hot((inner, inner * tile_cols), lambda i, j: j // tile_cols == i)
    return dot(dot(up, mask.astype(jnp.float32)), across)


def split(x):
    high = x.astype(jnp.bfloat16)
    return high, (x - high.astype(jnp.float32)).astype(jnp.bfloat16)


def dot_three(a, b, dims=(((1,), (0,)), ((), ()))):
    (a_high, a_low), (b_high, b_low) = a, b
    return dot(a_high, b_high, dims) + (dot(a_high, b_low, dims) + dot(a_low, b_high, dims))


def choose(place, values):
    picked = values[0]
    for at in range(1, len(values)):
        picked = jnp.where(place == at, values[at], picked)
    return picked


def other_rows(place, count):
    orders = [
        sorted((k for k in range(count) if k != at), key=lambda k: (abs(k - at) != 2, -abs(k - at), k))
        for at in range(count)
    ]
    return [
        (
            choose(place, [order[step] for order in orders]),
            choose(place, [abs(orders[at][step] - at) for at in range(count)]),
        )
        for step in range(count - 1)
    ]


def gather_kernel(
    rows, cols, int_hbm, occ_hbm, virt_hbm, imask_hbm, omask_hbm, vmask_hbm, out_ref,
    held, pair_high, pair_low, int_ref, occ_ref, virt_ref, imask_ref, omask_ref, vmask_ref,
    load_sem, send_sem, recv_sem
):
    basis, aux = int_ref.shape
    green_tile = basis // omask_ref.shape[0]
    highest = lax.Precision.HIGHEST
    group = lax.axis_index("groups")
    row = lax.axis_index("row")
    col = lax.axis_index("col")
    mate = col + 1 - 2 * (col % 2)
    across = (col + 2) % 4
    barrier = pltpu.get_barrier_semaphore()

    far = across + 1 - 2 * (across % 2)
    others = other_rows(row, rows)
    peers = [(group, other, col) for other, _ in others] + [(group, row, across), (group, row, mate)]
    for peer in peers:
        pl.semaphore_signal(barrier, inc=1, device_id=peer, device_id_type=MESH)
    greeted = len(peers)
    for other, away in others:

        @pl.when(away == 1)
        def _(other=other):
            pl.semaphore_signal(barrier, inc=1, device_id=(group, other, across), device_id_type=MESH)

        greeted = greeted + jnp.where(away == 1, 1, 0)

    sources = (imask_hbm.at[:, 0, :], int_hbm.at[:, 0, :], omask_hbm, vmask_hbm, occ_hbm, virt_hbm)
    targets = (imask_ref, int_ref, omask_ref, vmask_ref, occ_ref, virt_ref)
    loads = [
        pltpu.make_async_copy(source, target, load_sem.at[k])
        for k, (source, target) in enumerate(zip(sources, targets))
    ]
    for load in loads:
        load.start()
    loads[0].wait()
    mask = spread_tiles(imask_ref[...], green_tile, aux // imask_ref.shape[1])
    loads[1].wait()
    held[row * cols + col] = int_ref[...] * mask
    pl.semaphore_wait(barrier, greeted)

    def copy_of(block, peer, slot):
        return pltpu.make_async_remote_copy(
            src_ref=held.at[block],
            dst_ref=held.at[block],
            send_sem=send_sem.at[slot],
            recv_sem=recv_sem.at[block],
            device_id=peer,
            device_id_type=MESH,
        )

    def arrive(block):
        copy_of(block, (group, row, mate), 0).wait_recv()

    count = len(others)
    to_mate = 2 * count + 1

    def pass_on(block, slot):
        copy_of(block, (group, row, mate), to_mate + slot).start()

    mine = row * cols + col
    beside = row * cols + across
    copy_of(mine, (group, row, across), 2 * count).start()
    for step, (other, away) in enumerate(others):
        copy_of(mine, (group, other, col), step).start()
    for step, (other, away) in enumerate(others):

        @pl.when(away == 1)
        def _(other=other, step=step):
            copy_of(mine, (group, other, across), count + step).start()

    pass_on(mine, 0)

    for load in loads[2:]:
        load.wait()
    occ = occ_ref[...] * spread_tiles(omask_ref[...], green_tile, green_tile)
    virt = virt_ref[...] * spread_tiles(vmask_ref[...], green_tile, green_tile)
    wide = (basis, basis * basis)
    occ_cols = dot(occ, one_hot(wide, lambda i, j: j // basis == i), precision=highest)
    virt_cols = dot(
        virt, one_hot(wide, lambda i, j: j % basis == i), (((0,), (0,)), ((), ())), precision=highest
    )
    pair = (occ_cols[None] * virt_cols[:, None]).reshape(basis * basis, basis * basis) / basis
    high, low = split(pair)
    pair_high[...] = high
    pair_low[...] = low

    arrive(beside)
    for step, (other, away) in enumerate(others):

        @pl.when(away > 2)
        def _(other=other, step=step):
            copy_of(beside, (group, other, col), count + step).start()

    pass_on(beside, 1)
    for step, (other, away) in enumerate(others):
        block = other * cols + col
        arrive(block)

        @pl.when(away == 2)
        def _(block=block, step=step):
            copy_of(block, (group, row, across), count + step).start()

        pass_on(block, 2 + step)
    for step, (other, away) in reversed(list(enumerate(others))):
        block = other * cols + across
        arrive(block)
        pass_on(block, 2 + count + step)
    arrive(row * cols + mate)
    arrive(row * cols + far)
    for other, _ in others:
        arrive(other * cols + mate)
    for other, _ in others:
        arrive(other * cols + far)
    for slot in range(to_mate + 2 * rows):
        copy_of(mine, (group, row, mate), slot).wait_send()

    mine_out = out_ref.shape[0]
    begin = pl.multiple_of(row * mine_out, mine_out)
    left = held[:, :, pl.ds(begin, mine_out)].reshape(basis * basis, mine_out)
    turned = dot_three(split(left.T), (pair_high[...], pair_low[...]))
    whole = split(held[...].reshape(basis * basis, aux))
    out_ref[...] = dot_three(split(turned), whole)


def gather_plan(integrals, occupied, virtual, int_mask, occ_mask, virt_mask):
    basis, _, aux = integrals.shape
    rows, cols = lax.axis_size("row"), lax.axis_size("col")
    anywhere = pl.BlockSpec(memory_space=pl.ANY)
    return pl.pallas_call(
        functools.partial(gather_kernel, rows, cols),
        out_shape=pltpu.VMEM((aux // rows, aux), jnp.float32),
        in_specs=[anywhere] * 6,
        out_specs=pl.BlockSpec(memory_space=pltpu.VMEM),
        scratch_shapes=[
            pltpu.VMEM((basis, basis, aux), jnp.float32),
            pltpu.VMEM((basis * basis, basis * basis), jnp.bfloat16),
            pltpu.VMEM((basis * basis, basis * basis), jnp.bfloat16),
            pltpu.VMEM((basis, aux), jnp.float32),
            pltpu.VMEM(occupied.shape, jnp.float32),
            pltpu.VMEM(virtual.shape, jnp.float32),
            pltpu.VMEM((int_mask.shape[0], int_mask.shape[2]), jnp.int32),
            pltpu.VMEM(occ_mask.shape, jnp.int32),
            pltpu.VMEM(virt_mask.shape, jnp.int32),
            pltpu.SemaphoreType.DMA((6,)),
            pltpu.SemaphoreType.DMA((4 * rows - 1,)),
            pltpu.SemaphoreType.DMA((rows * cols,)),
        ],
        compiler_params=pltpu.CompilerParams(collective_id=0, has_side_effects=True),
    )(integrals, occupied, virtual, int_mask, occ_mask, virt_mask)


def per_device(integrals, occupied, virtual, int_mask, occ_mask, virt_mask):
    basis, local_pairs, aux = integrals.shape
    rows, cols = lax.axis_size("row"), lax.axis_size("col")
    small = local_pairs == 1 and cols == 4 and rows * cols == basis
    fits = basis * basis * (aux + basis * basis) * 4 <= 16 * 1024 * 1024
    tiled = basis % 8 == 0 and aux % (128 * rows) == 0
    plan = gather_plan if small and fits and tiled else exchange_plan
    return plan(integrals, occupied, virtual, int_mask, occ_mask, virt_mask)


def solution(mesh):
    placed = (
        P("groups", ("row", "col"), None),
        P("groups", None),
        P("groups", None),
        P("groups", ("row", "col"), None),
        P("groups", None),
        P("groups", None),
    )
    return jax.shard_map(
        per_device,
        mesh=mesh,
        in_specs=placed,
        out_specs=P(("groups", "row"), None),
        check_vma=False,
    )
```

```python
import functools

import jax
import jax.numpy as jnp
from jax import lax
from jax.experimental import pallas as pl
from jax.experimental.pallas import tpu as pltpu
from jax.sharding import PartitionSpec as P

MESH = pl.DeviceIdType.MESH


def spread_two(mask, tile_rows, tile_cols):
    outer, inner = mask.shape
    wide = jnp.broadcast_to(mask[:, None, :, None], (outer, tile_rows, inner, tile_cols))
    return wide.reshape(outer * tile_rows, inner * tile_cols).astype(jnp.float32)


def spread_three(mask, tile_rows, tile_cols):
    outer, middle, inner = mask.shape
    wide = jnp.broadcast_to(mask[:, None, :, :, None], (outer, tile_rows, middle, inner, tile_cols))
    return wide.reshape(outer * tile_rows, middle, inner * tile_cols).astype(jnp.float32)


def exchange_plan(integrals, occupied, virtual, int_mask, occ_mask, virt_mask):
    highest = lax.Precision.HIGHEST
    basis = occupied.shape[0]
    local_pairs = integrals.shape[1]
    aux_count = integrals.shape[2]
    green_tile = basis // occ_mask.shape[0]
    aux_tile = aux_count // int_mask.shape[2]
    row_count = lax.axis_size("row")
    col_count = lax.axis_size("col")
    int_full = integrals * spread_three(int_mask, green_tile, aux_tile)
    occ_full = occupied * spread_two(occ_mask, green_tile, green_tile)
    virt_full = virtual * spread_two(virt_mask, green_tile, green_tile)
    flat = int_full.reshape(basis, local_pairs * aux_count)
    contract_first = (((0,), (0,)), ((), ()))
    trans_virt = lax.dot_general(
        virt_full, flat, contract_first, precision=highest, preferred_element_type=jnp.float32
    )
    shaped_virt = trans_virt.reshape(row_count, col_count, local_pairs, local_pairs, aux_count)
    mirrored = lax.all_to_all(
        lax.all_to_all(shaped_virt, "row", split_axis=0, concat_axis=0, tiled=True),
        "col",
        split_axis=1,
        concat_axis=1,
        tiled=True,
    )
    trans_occ = lax.dot_general(
        occ_full, flat, contract_first, precision=highest, preferred_element_type=jnp.float32
    )
    shaped_occ = trans_occ.reshape(row_count, col_count, local_pairs, local_pairs, aux_count)
    pair_dims = (((0, 1, 2, 3), (0, 1, 3, 2)), ((), ()))
    whole = (
        lax.dot_general(
            shaped_occ, mirrored, pair_dims, precision=highest, preferred_element_type=jnp.float32
        )
        / basis
    )
    summed = lax.psum(whole, "col")
    return lax.psum_scatter(summed, "row", scatter_dimension=0, tiled=True)


def one_hot(shape, which):
    rows = lax.broadcasted_iota(jnp.int32, shape, 0)
    cols = lax.broadcasted_iota(jnp.int32, shape, 1)
    return jnp.where(which(rows, cols), 1.0, 0.0).astype(jnp.float32)


def dot(a, b, dims=(((1,), (0,)), ((), ())), precision=None):
    return lax.dot_general(a, b, dims, precision=precision, preferred_element_type=jnp.float32)


def spread_tiles(mask, tile_rows, tile_cols):
    outer, inner = mask.shape
    up = one_hot((outer * tile_rows, outer), lambda i, j: i // tile_rows == j)
    across = one_hot((inner, inner * tile_cols), lambda i, j: j // tile_cols == i)
    return dot(dot(up, mask.astype(jnp.float32)), across)


def split(x):
    high = x.astype(jnp.bfloat16)
    return high, (x - high.astype(jnp.float32)).astype(jnp.bfloat16)


def dot_three(a, b, dims=(((1,), (0,)), ((), ()))):
    (a_high, a_low), (b_high, b_low) = a, b
    return dot(a_high, b_high, dims) + (dot(a_high, b_low, dims) + dot(a_low, b_high, dims))


def choose(place, values):
    picked = values[0]
    for at in range(1, len(values)):
        picked = jnp.where(place == at, values[at], picked)
    return picked


def other_rows(place, count):
    orders = [
        sorted((k for k in range(count) if k != at), key=lambda k: (abs(k - at) != 2, -abs(k - at), k))
        for at in range(count)
    ]
    return [
        (
            choose(place, [order[step] for order in orders]),
            choose(place, [abs(orders[at][step] - at) for at in range(count)]),
        )
        for step in range(count - 1)
    ]


def gather_kernel(
    rows, cols, int_hbm, occ_hbm, virt_hbm, imask_hbm, omask_hbm, vmask_hbm, out_ref,
    held, pair_high, pair_low, int_ref, occ_ref, virt_ref, imask_ref, omask_ref, vmask_ref,
    load_sem, send_sem, recv_sem
):
    basis, aux = int_ref.shape
    green_tile = basis // omask_ref.shape[0]
    highest = lax.Precision.HIGHEST
    group = lax.axis_index("groups")
    row = lax.axis_index("row")
    col = lax.axis_index("col")
    mate = col + 1 - 2 * (col % 2)
    across = (col + 2) % 4
    barrier = pltpu.get_barrier_semaphore()

    far = across + 1 - 2 * (across % 2)
    others = other_rows(row, rows)
    peers = [(group, other, col) for other, _ in others] + [(group, row, across), (group, row, mate)]
    for peer in peers:
        pl.semaphore_signal(barrier, inc=1, device_id=peer, device_id_type=MESH)
    greeted = len(peers)
    for other, away in others:

        @pl.when(away == 1)
        def _(other=other):
            pl.semaphore_signal(barrier, inc=1, device_id=(group, other, across), device_id_type=MESH)

        greeted = greeted + jnp.where(away == 1, 1, 0)

    sources = (imask_hbm.at[:, 0, :], int_hbm.at[:, 0, :], omask_hbm, vmask_hbm, occ_hbm, virt_hbm)
    targets = (imask_ref, int_ref, omask_ref, vmask_ref, occ_ref, virt_ref)
    loads = [
        pltpu.make_async_copy(source, target, load_sem.at[k])
        for k, (source, target) in enumerate(zip(sources, targets))
    ]
    for load in loads:
        load.start()
    loads[0].wait()
    mask = spread_tiles(imask_ref[...], green_tile, aux // imask_ref.shape[1])
    loads[1].wait()
    held[row * cols + col] = int_ref[...] * mask
    for load in loads[2:]:
        load.wait()
    occ = occ_ref[...] * spread_tiles(omask_ref[...], green_tile, green_tile)
    virt = virt_ref[...] * spread_tiles(vmask_ref[...], green_tile, green_tile)
    wide = (basis, basis * basis)
    occ_cols = dot(occ, one_hot(wide, lambda i, j: j // basis == i), precision=highest)
    virt_cols = dot(
        virt, one_hot(wide, lambda i, j: j % basis == i), (((0,), (0,)), ((), ())), precision=highest
    )
    pair = (occ_cols[None] * virt_cols[:, None]).reshape(basis * basis, basis * basis) / basis
    high, low = split(pair)
    pair_high[...] = high
    pair_low[...] = low
    pl.semaphore_wait(barrier, greeted)

    def copy_of(block, peer, slot):
        return pltpu.make_async_remote_copy(
            src_ref=held.at[block],
            dst_ref=held.at[block],
            send_sem=send_sem.at[slot],
            recv_sem=recv_sem.at[block],
            device_id=peer,
            device_id_type=MESH,
        )

    def arrive(block):
        copy_of(block, (group, row, mate), 0).wait_recv()

    count = len(others)
    to_mate = 2 * count + 1

    def pass_on(block, slot):
        copy_of(block, (group, row, mate), to_mate + slot).start()

    mine = row * cols + col
    beside = row * cols + across
    copy_of(mine, (group, row, across), 2 * count).start()
    for step, (other, away) in enumerate(others):
        copy_of(mine, (group, other, col), step).start()
    for step, (other, away) in enumerate(others):

        @pl.when(away == 1)
        def _(other=other, step=step):
            copy_of(mine, (group, other, across), count + step).start()

    pass_on(mine, 0)


    arrive(beside)
    for step, (other, away) in enumerate(others):

        @pl.when(away > 2)
        def _(other=other, step=step):
            copy_of(beside, (group, other, col), count + step).start()

    pass_on(beside, 1)
    for step, (other, away) in enumerate(others):
        block = other * cols + col
        arrive(block)

        @pl.when(away == 2)
        def _(block=block, step=step):
            copy_of(block, (group, row, across), count + step).start()

        pass_on(block, 2 + step)
    for step, (other, away) in reversed(list(enumerate(others))):
        block = other * cols + across
        arrive(block)
        pass_on(block, 2 + count + step)
    arrive(row * cols + mate)
    arrive(row * cols + far)
    for other, _ in others:
        arrive(other * cols + mate)
    for other, _ in others:
        arrive(other * cols + far)
    for slot in range(to_mate + 2 * rows):
        copy_of(mine, (group, row, mate), slot).wait_send()

    mine_out = out_ref.shape[0]
    begin = pl.multiple_of(row * mine_out, mine_out)
    left = held[:, :, pl.ds(begin, mine_out)].reshape(basis * basis, mine_out)
    turned = dot_three(split(left.T), (pair_high[...], pair_low[...]))
    whole = split(held[...].reshape(basis * basis, aux))
    out_ref[...] = dot_three(split(turned), whole)


def gather_plan(integrals, occupied, virtual, int_mask, occ_mask, virt_mask):
    basis, _, aux = integrals.shape
    rows, cols = lax.axis_size("row"), lax.axis_size("col")
    anywhere = pl.BlockSpec(memory_space=pl.ANY)
    return pl.pallas_call(
        functools.partial(gather_kernel, rows, cols),
        out_shape=pltpu.VMEM((aux // rows, aux), jnp.float32),
        in_specs=[anywhere] * 6,
        out_specs=pl.BlockSpec(memory_space=pltpu.VMEM),
        scratch_shapes=[
            pltpu.VMEM((basis, basis, aux), jnp.float32),
            pltpu.VMEM((basis * basis, basis * basis), jnp.bfloat16),
            pltpu.VMEM((basis * basis, basis * basis), jnp.bfloat16),
            pltpu.VMEM((basis, aux), jnp.float32),
            pltpu.VMEM(occupied.shape, jnp.float32),
            pltpu.VMEM(virtual.shape, jnp.float32),
            pltpu.VMEM((int_mask.shape[0], int_mask.shape[2]), jnp.int32),
            pltpu.VMEM(occ_mask.shape, jnp.int32),
            pltpu.VMEM(virt_mask.shape, jnp.int32),
            pltpu.SemaphoreType.DMA((6,)),
            pltpu.SemaphoreType.DMA((4 * rows - 1,)),
            pltpu.SemaphoreType.DMA((rows * cols,)),
        ],
        compiler_params=pltpu.CompilerParams(collective_id=0, has_side_effects=True),
    )(integrals, occupied, virtual, int_mask, occ_mask, virt_mask)


def per_device(integrals, occupied, virtual, int_mask, occ_mask, virt_mask):
    basis, local_pairs, aux = integrals.shape
    rows, cols = lax.axis_size("row"), lax.axis_size("col")
    small = local_pairs == 1 and cols == 4 and rows * cols == basis
    fits = basis * basis * (aux + basis * basis) * 4 <= 16 * 1024 * 1024
    tiled = basis % 8 == 0 and aux % (128 * rows) == 0
    plan = gather_plan if small and fits and tiled else exchange_plan
    return plan(integrals, occupied, virtual, int_mask, occ_mask, virt_mask)


def solution(mesh):
    placed = (
        P("groups", ("row", "col"), None),
        P("groups", None),
        P("groups", None),
        P("groups", ("row", "col"), None),
        P("groups", None),
        P("groups", None),
    )
    return jax.shard_map(
        per_device,
        mesh=mesh,
        in_specs=placed,
        out_specs=P(("groups", "row"), None),
        check_vma=False,
    )
```
